32 devices in a mesh: row: 8 (over z, x), col: 2 (over y), snode: 2 (over core).
Axes of the slice: x: 2, y: 2, z: 4, core: 2. Of those that a mesh axis runs over, the one named last changes fastest.
Arguments:
- ancestor_inverse: bfloat16 [40960, 20480], P(('snode', 'row'), 'col'), parts along dimension 0, may hold values from -8 to 8
- fill_mask: int32 [160, 80], P('snode'), parts along dimension 0, may hold values from 0 to 1, as said below
- block_order: int32 [4, 80], P('snode'), parts along dimension 0, may hold values from 0 to 79, each once within a row
- l_rows: bfloat16 [4, 20480, 256], P('snode', ('row', 'col')), parts along dimension 0, may hold values from -6 to 6
- diag_inverse: bfloat16 [4, 256, 256], P('snode'), parts along dimension 0, may hold values from -0.0024414062 to 0.0024414062
Outputs:
- ainv_kr: bfloat16 [4, 256, 20480], P('snode', None, ('row', 'col')), parts along dimension 0
The draws below stay inside these ranges and needn't reach their ends.
There are 2 independent parts, one for each index of `snode`. The reference program is written for one: setup_inputs(seed, part) draws one part's arguments, and reference() takes and returns one part's arrays. A program takes and returns all parts, laid end to end along the dimension named above; each array names one. Nothing has to cross between parts.
Inputs may be any that keep to these rules, and one draw needn't show every extreme that they name: Tile (i, j) takes part exactly where fill_mask is 1; diagonal tiles are always 1. `block_order`: each row is a permutation of the 80 ancestor blocks.
All inputs are finite; a program needn't handle non-finite values.
Results may differ from the reference program's by a relative error of at most 0.014.
Values may be sent and summed in bfloat16 or wider, within the bound.
A program may use at most 256 MiB of HBM per device.

```python
import jax
import jax.numpy as jnp
from jax import lax

TILE = 256
BLOCKS = 80
SNODES = 2
ORDER = 20480


def draw_fill_mask(key, part):
    sub_key = jax.random.fold_in(key, 11)
    row_ids = jnp.arange(BLOCKS, dtype=jnp.int32)[:, None]
    col_ids = jnp.arange(BLOCKS, dtype=jnp.int32)[None, :]
    threshold = 20 + 80 * row_ids // (BLOCKS - 1)
    drawn_value = jax.random.randint(sub_key, (BLOCKS, BLOCKS), 0, 100)
    filled = jnp.where(drawn_value < threshold, 1, 0)
    return jnp.where(row_ids == col_ids, 1, filled).astype(jnp.int32)


def levels(rng, shape, split, smallest, top_value):
    factor_of = 1.0
    for position, blocks in split:
        heights = jax.random.uniform(jax.random.fold_in(jax.random.fold_in(rng, 6), position), (blocks,), jnp.float32, smallest / len(split), top_value / len(split))
        factor_of = factor_of * jnp.repeat(jnp.exp(heights), shape[position] // blocks).reshape((-1,) + (1,) * (len(shape) - 1 - position))
    return factor_of


def gaussian(stream_key, dims, width, reach, cuts=(), held_as=jnp.bfloat16):
    loudness = levels(stream_key, dims, cuts, -0.22, 0.18) if cuts else 1.0
    drawn = jax.random.normal(stream_key, dims, jnp.float32) * width * loudness
    return jnp.minimum(jnp.maximum(drawn, -reach), reach).astype(held_as)


def setup_inputs(seed: int = 0, part: int = 0) -> dict:
    keys = jax.random.split(jax.random.key(seed), 6)
    part_splits = jax.random.split(jax.random.fold_in(keys[5], part), 6)
    ancestor_inverse = gaussian(part_splits[0], (ORDER, ORDER), 1.3, 8.0, ((0, 8), (1, 2)))
    fill_mask = draw_fill_mask(jax.random.fold_in(jax.random.fold_in(keys[5], part), 71), part)
    block_order = jax.vmap(lambda own: jax.random.permutation(own, BLOCKS))(jax.random.split(part_splits[2], SNODES)).reshape((SNODES, BLOCKS)).astype(jnp.int32)
    l_rows = gaussian(part_splits[3], (SNODES, ORDER, TILE), 1.0, 6.0, ((1, 16),))
    diag_inverse = gaussian(part_splits[4], (SNODES, TILE, TILE), (BLOCKS * TILE * TILE) ** -0.5, 0.0024414062)
    return dict(ancestor_inverse=ancestor_inverse, fill_mask=fill_mask, block_order=block_order, l_rows=l_rows, diag_inverse=diag_inverse)


def reference(ancestor_inverse, fill_mask, block_order, l_rows, diag_inverse):
    snode_count = diag_inverse.shape[0]
    tile_size = diag_inverse.shape[1]
    block_count = fill_mask.shape[0]
    normed = jnp.einsum("sxy,syz->sxz", l_rows.astype(jnp.float32), diag_inverse.astype(jnp.float32), precision=lax.Precision.HIGHEST).astype(jnp.bfloat16)
    pieces = normed.reshape(snode_count, block_count, tile_size, tile_size).astype(jnp.float32)
    targets = jnp.arange(block_count, dtype=jnp.int32)
    selector = (block_order[:, None, :] == targets[None, :, None]).astype(jnp.float32)
    aligned = jnp.einsum("saq,sqxy->saxy", selector, pieces, precision=lax.Precision.HIGHEST)
    stacked = aligned.transpose(1, 2, 0, 3).reshape(block_count * tile_size, snode_count * tile_size)

    def one_row(block_id):
        row_slab = lax.dynamic_slice_in_dim(ancestor_inverse, block_id * tile_size, tile_size, 0).astype(jnp.float32)
        row_gate = jnp.repeat(lax.dynamic_slice_in_dim(fill_mask, block_id, 1, 0)[0].astype(jnp.float32), tile_size)
        return -jnp.dot(row_slab * row_gate[None, :], stacked, precision=lax.Precision.HIGHEST)

    product = lax.map(one_row, jnp.arange(block_count, dtype=jnp.int32))
    product = product.reshape(block_count * tile_size, snode_count, tile_size)
    return product.transpose(1, 2, 0).astype(jnp.bfloat16)
```

```python
import functools

import jax
import jax.numpy as jnp
from jax import lax
from jax.experimental import pallas as pl
from jax.experimental.pallas import tpu as pltpu
from jax.sharding import PartitionSpec as P

MESH = pl.DeviceIdType.MESH
UP, DOWN, XP, YP = range(4)


def gather_plan(blocks):
    fifth = blocks // 5
    half = max(fifth, 1)
    plan = []
    start = 0
    for order, share in (("zxy", 2 * fifth), ("zyx", 2 * fifth), ("xyz", fifth // 2)):
        while share > 0:
            size = min(half, share)
            plan.append((start, size, order))
            start += size
            share -= size
    while start < blocks:
        size = min(half, blocks - start)
        size = min(size, max(fifth // 2, 1))
        plan.append((start, size, "yxz"))
        start += size
    rank = {"zxy": 0, "zyx": 1, "xyz": 2, "yxz": 3}
    count = {}
    keyed = []
    for piece in plan:
        n = count.get(piece[2], 0)
        count[piece[2]] = n + 1
        keyed.append((n, rank[piece[2]], piece))
    return [piece for _, _, piece in sorted(keyed)]


def gather_kernel(depth, plan, own_ref, out_ref, send_sem, recv_sem, local_sem):
    row = lax.axis_index("row")
    y = lax.axis_index("col")
    core = lax.axis_index("snode")
    z = row // 2
    x = row % 2
    where = {
        UP: ((z + 1) * 2 + x, y, core),
        DOWN: ((z - 1) * 2 + x, y, core),
        XP: (z * 2 + 1 - x, y, core),
        YP: (row, 1 - y, core),
    }
    exists = {UP: z + 1 < depth, DOWN: z >= 1}

    barrier = pltpu.get_barrier_semaphore()
    for way in (XP, YP):
        pl.semaphore_signal(barrier, inc=1, device_id=where[way], device_id_type=MESH)
    for way in (UP, DOWN):

        @pl.when(exists[way])
        def _():
            pl.semaphore_signal(barrier, inc=1, device_id=where[way], device_id_type=MESH)

    ends = (depth > 1) + (depth > 2)
    inner = jnp.logical_and(exists[UP], exists[DOWN])

    @pl.when(inner)
    def _():
        pl.semaphore_wait(barrier, 2 + ends)

    @pl.when(jnp.logical_not(inner))
    def _():
        pl.semaphore_wait(barrier, 2 + (depth > 1))

    me = row * 2 + y

    def slot_of(zz, xx, yy):
        return (zz * 2 + xx) * 2 + yy

    sent = []

    def descriptor(number, slot, own, way, target=None):
        start, size, _ = plan[number]
        span = pl.ds(start, size)
        source = own_ref.at[span] if own else out_ref.at[slot, span]
        return pltpu.make_async_remote_copy(
            src_ref=source,
            dst_ref=out_ref.at[slot, span],
            send_sem=send_sem.at[way, slot, number],
            recv_sem=recv_sem.at[slot, number],
            device_id=where[way] if target is None else target,
            device_id_type=MESH,
        )

    def guarded(cond, fn):
        if cond is None:
            fn()
        else:
            pl.when(cond)(fn)

    def both(a, b):
        if a is None:
            return b
        if b is None:
            return a
        return jnp.logical_and(a, b)

    def send(number, slot, own, way, cond):
        cond = both(cond, exists.get(way))
        guarded(cond, lambda: descriptor(number, slot, own, way).start())
        sent.append((number, slot, own, way, cond))

    def arrived(number, slot, cond):
        guarded(cond, lambda: descriptor(number, slot, False, XP).wait_recv())

    local = pltpu.make_async_copy(own_ref, out_ref.at[me], local_sem)
    local.start()

    partner = {"x": XP, "y": YP}

    def coords(flip_x, flip_y):
        return (1 - x if flip_x else x), (1 - y if flip_y else y)

    reach = [0]
    for k in range(1, depth):
        reach += [-k, k]

    def near(dz):
        if dz == 0:
            return None
        return z + dz >= 0 if dz < 0 else z + dz < depth

    def onward_z(number, slot, own, dz, cond):
        if dz <= 0:
            send(number, slot, own, UP, cond)
        if dz >= 0:
            send(number, slot, own, DOWN, cond)

    def z_first(number, order, dz, level):
        first, second = order[1], order[2]
        flips = {0: "", 1: first, 2: second, 3: "xy"}[level]
        xx, yy = coords("x" in flips, "y" in flips)
        slot = slot_of(z + dz, xx, yy)
        own = level == 0 and dz == 0
        cond = near(dz)
        if not own:
            arrived(number, slot, cond)
        if level == 0:
            onward_z(number, slot, own, dz, cond)
            send(number, slot, own, partner[first], cond)
            send(number, slot, own, partner[second], cond)
        elif level == 1:
            send(number, slot, own, partner[second], cond)

    def z_last(number, order, dz, level):
        first, second = order[0], order[1]
        flips = {0: "", 1: first, 2: second, 3: "xy"}[level]
        xx, yy = coords("x" in flips, "y" in flips)
        slot = slot_of(z + dz, xx, yy)
        own = level == 0 and dz == 0
        cond = near(dz)
        if not own:
            arrived(number, slot, cond)
        onward_z(number, slot, own, dz, cond)
        if dz == 0:
            if level == 0:
                send(number, slot, own, partner[first], cond)
            if level in (0, 1):
                send(number, slot, own, partner[second], cond)

    def handle(number, dz, level):
        order = plan[number][2]
        (z_first if order[0] == "z" else z_last)(number, order, dz, level)

    numbers = range(len(plan))
    events = []
    for number in numbers:
        for position, dz in enumerate(reach):
            hop = (position + 1) // 2
            for level in range(4):
                events.append((2 * hop + (0, 1, 1, 2)[level], number, position, level, dz))
    events.sort(key=lambda e: e[:4])
    for _, number, _, level, dz in events:
        handle(number, dz, level)
    for number, slot, own, way, cond in sent:
        guarded(cond, lambda: descriptor(number, slot, own, way).wait_send())
    local.wait()


def gather(own, row_size, col_size):
    depth = row_size // 2
    blocks = own.shape[0]
    plan = gather_plan(blocks)
    devices = row_size * col_size
    return pl.pallas_call(
        functools.partial(gather_kernel, depth, plan),
        out_shape=jax.ShapeDtypeStruct((devices,) + own.shape, own.dtype),
        in_specs=[pl.BlockSpec(memory_space=pl.ANY)],
        out_specs=pl.BlockSpec(memory_space=pl.ANY),
        scratch_shapes=[
            pltpu.SemaphoreType.DMA((4, devices, len(plan))),
            pltpu.SemaphoreType.DMA((devices, len(plan))),
            pltpu.SemaphoreType.DMA,
        ],
        compiler_params=pltpu.CompilerParams(collective_id=0, has_side_effects=True),
        name="gather",
    )(own)


def product_kernel(snodes, width, tile, table_ref, gate_ref, half_ref, a_ref, *rest):
    piece_refs = rest[: snodes * width]
    out_ref, stack_ref, total_ref = rest[snodes * width :]
    step = pl.program_id(0)
    for b in range(width):
        for s in range(snodes):
            stack_ref[b * tile : (b + 1) * tile, s * tile : (s + 1) * tile] = piece_refs[
                b * snodes + s
            ][...]

    @pl.when(step == 0)
    def _():
        total_ref[...] = jnp.zeros_like(total_ref)

    row_tiles = a_ref.shape[0] // tile
    for i in range(row_tiles):
        rows = slice(i * tile, (i + 1) * tile)
        parts = []
        for b in range(width):
            gate = gate_ref[half_ref[0] * row_tiles + i, step * width + b]
            part = a_ref[rows, b * tile : (b + 1) * tile]
            parts.append(part * gate.astype(jnp.float32).astype(part.dtype))
        total_ref[rows, :] += jnp.dot(
            jnp.concatenate(parts, axis=1), stack_ref[...], preferred_element_type=jnp.float32
        )

    @pl.when(step == pl.num_programs(0) - 1)
    def _():
        for i in range(row_tiles):
            rows = slice(i * tile, (i + 1) * tile)
            out_ref[:, rows] = (-total_ref[rows, :]).T.astype(out_ref.dtype)


def product(table, gate, half, ancestor_inverse, pieces, shares, snodes, tile, dtype):
    local_rows, local_cols = ancestor_inverse.shape
    rows = local_rows // shares
    col_blocks = local_cols // tile
    width = max(w for w in range(1, 6) if col_blocks % w == 0)

    def piece_spec(b, s):
        return pl.BlockSpec(
            (pl.Squeezed(), tile, tile),
            lambda k, table_ref, gate_ref, half_ref: (table_ref[s, k * width + b], 0, 0),
        )

    return pl.pallas_call(
        functools.partial(product_kernel, snodes, width, tile),
        out_shape=jax.ShapeDtypeStruct((snodes * tile, rows), dtype),
        grid_spec=pltpu.PrefetchScalarGridSpec(
            num_scalar_prefetch=3,
            grid=(col_blocks // width,),
            in_specs=[
                pl.BlockSpec((rows, width * tile), lambda k, t, g, half_ref: (half_ref[0], k))
            ]
            + [piece_spec(b, s) for b in range(width) for s in range(snodes)],
            out_specs=pl.BlockSpec((snodes * tile, rows), lambda k, t, g, h: (0, 0)),
            scratch_shapes=[
                pltpu.VMEM((width * tile, snodes * tile), jnp.bfloat16),
                pltpu.VMEM((rows, snodes * tile), jnp.float32),
            ],
        ),
        compiler_params=pltpu.CompilerParams(
            dimension_semantics=("arbitrary",), vmem_limit_bytes=56 * 1024 * 1024
        ),
        cost_estimate=pl.CostEstimate(
            flops=2 * rows * local_cols * snodes * tile,
            bytes_accessed=2 * rows * local_cols,
            transcendentals=0,
        ),
        name="product",
    )(table, gate, half, ancestor_inverse, *([pieces] * (snodes * width)))


def fast(ancestor_inverse, fill_mask, block_order, l_rows, diag_inverse):
    row_index = lax.axis_index("row")
    col_index = lax.axis_index("col")
    row_size = lax.axis_size("row")
    col_size = lax.axis_size("col")
    local_rows, local_cols = ancestor_inverse.shape
    snodes, tile = diag_inverse.shape[:2]
    row_blocks = local_rows // tile
    col_blocks = local_cols // tile
    held = l_rows.shape[1] // tile
    normed = jnp.einsum(
        "sxy,syz->sxz", l_rows, diag_inverse, preferred_element_type=jnp.float32
    ).astype(jnp.bfloat16)
    own = normed.reshape(snodes * held, tile, tile)
    pieces = gather(own, row_size, col_size).reshape(-1, tile, tile)

    wanted = col_index * col_blocks + jnp.arange(col_blocks, dtype=jnp.int32)
    packed = jnp.arange(block_order.shape[1], dtype=jnp.int32)
    place = jnp.sum(
        jnp.where(block_order[:, None, :] == wanted[None, :, None], packed[None, None, :], 0), axis=2
    )
    table = (
        (place // held) * (snodes * held)
        + jnp.arange(snodes, dtype=jnp.int32)[:, None] * held
        + place % held
    ).astype(jnp.int32)
    gate = lax.dynamic_slice(
        fill_mask, (row_index * row_blocks, col_index * col_blocks), (row_blocks, col_blocks)
    )

    def share(half, dtype):
        return product(
            table, gate, half.reshape(1).astype(jnp.int32), ancestor_inverse, pieces,
            col_size, snodes, tile, dtype,
        )

    theirs = share(1 - col_index, jnp.bfloat16)
    received = lax.ppermute(theirs, "col", [(0, 1), (1, 0)])
    mine = share(col_index, jnp.float32)
    total = (mine + received.astype(jnp.float32)).astype(jnp.bfloat16)
    return total.reshape(snodes, tile, local_rows // col_size)


def plain(ancestor_inverse, fill_mask, block_order, l_rows, diag_inverse):
    row_index = lax.axis_index("row")
    col_index = lax.axis_index("col")
    local_rows, local_cols = ancestor_inverse.shape
    snode_count, tile_size = diag_inverse.shape[:2]
    block_count = fill_mask.shape[0]
    row_blocks = local_rows // tile_size
    col_blocks = local_cols // tile_size
    normed = jnp.einsum(
        "sxy,syz->sxz", l_rows, diag_inverse, preferred_element_type=jnp.float32
    ).astype(jnp.bfloat16)
    wanted = col_index * col_blocks + jnp.arange(col_blocks, dtype=jnp.int32)
    everything = lax.all_gather(normed, ("row", "col"), axis=1, tiled=True)
    pieces = everything.reshape(snode_count, block_count, tile_size, tile_size)
    selector = (block_order[:, None, :] == wanted[None, :, None]).astype(jnp.bfloat16)
    columns = jnp.einsum(
        "saq,sqxy->saxy", selector, pieces, preferred_element_type=jnp.float32
    ).astype(jnp.bfloat16)
    stacked = columns.transpose(1, 2, 0, 3).reshape(local_cols, snode_count * tile_size)
    tile_gate = lax.dynamic_slice(
        fill_mask, (row_index * row_blocks, col_index * col_blocks), (row_blocks, col_blocks)
    ).astype(jnp.bfloat16)
    masked = (
        ancestor_inverse.reshape(row_blocks, tile_size, col_blocks, tile_size)
        * tile_gate[:, None, :, None]
    ).reshape(local_rows, local_cols)
    share_rows = local_rows // lax.axis_size("col")
    own_rows = lax.psum_scatter(
        (-jnp.dot(masked, stacked, preferred_element_type=jnp.float32)).astype(jnp.bfloat16),
        "col",
        scatter_dimension=0,
        tiled=True,
    ).astype(jnp.float32)
    return (
        own_rows.reshape(share_rows, snode_count, tile_size).transpose(1, 2, 0).astype(jnp.bfloat16)
    )


def per_device(ancestor_inverse, fill_mask, block_order, l_rows, diag_inverse):
    tile = diag_inverse.shape[1]
    col_size = lax.axis_size("col")
    if (
        col_size == 2
        and lax.axis_size("row") % 2 == 0
        and l_rows.shape[1] % tile == 0
        and ancestor_inverse.shape[0] % (col_size * tile) == 0
    ):
        return fast(ancestor_inverse, fill_mask, block_order, l_rows, diag_inverse)
    return plain(ancestor_inverse, fill_mask, block_order, l_rows, diag_inverse)


def solution(mesh):
    return jax.shard_map(
        per_device,
        mesh=mesh,
        in_specs=(
            P(("snode", "row"), "col"),
            P("snode", None),
            P("snode", None),
            P("snode", ("row", "col"), None),
            P("snode", None, None),
        ),
        out_specs=P("snode", None, ("row", "col")),
        check_vma=False,
    )
```

```python
import functools

import jax
import jax.numpy as jnp
from jax import lax
from jax.experimental import pallas as pl
from jax.experimental.pallas import tpu as pltpu
from jax.sharding import PartitionSpec as P

MESH = pl.DeviceIdType.MESH
UP, DOWN, XP, YP = range(4)


def gather_plan(blocks):
    fifth = blocks // 5
    half = max(fifth, 1)
    plan = []
    start = 0
    for order, share in (("zxy", 2 * fifth), ("zyx", 2 * fifth), ("xyz", fifth // 2)):
        while share > 0:
            size = min(half, share)
            plan.append((start, size, order))
            start += size
            share -= size
    while start < blocks:
        size = min(half, blocks - start)
        size = min(size, max(fifth // 2, 1))
        plan.append((start, size, "yxz"))
        start += size
    rank = {"zxy": 0, "zyx": 1, "xyz": 2, "yxz": 3}
    count = {}
    keyed = []
    for piece in plan:
        n = count.get(piece[2], 0)
        count[piece[2]] = n + 1
        keyed.append((n, rank[piece[2]], piece))
    return [piece for _, _, piece in sorted(keyed)]


def gather_kernel(depth, plan, own_ref, out_ref, send_sem, recv_sem, local_sem):
    row = lax.axis_index("row")
    y = lax.axis_index("col")
    core = lax.axis_index("snode")
    z = row // 2
    x = row % 2
    where = {
        UP: ((z + 1) * 2 + x, y, core),
        DOWN: ((z - 1) * 2 + x, y, core),
        XP: (z * 2 + 1 - x, y, core),
        YP: (row, 1 - y, core),
    }
    exists = {UP: z + 1 < depth, DOWN: z >= 1}

    barrier = pltpu.get_barrier_semaphore()
    for way in (XP, YP):
        pl.semaphore_signal(barrier, inc=1, device_id=where[way], device_id_type=MESH)
    for way in (UP, DOWN):

        @pl.when(exists[way])
        def _():
            pl.semaphore_signal(barrier, inc=1, device_id=where[way], device_id_type=MESH)

    ends = (depth > 1) + (depth > 2)
    inner = jnp.logical_and(exists[UP], exists[DOWN])

    @pl.when(inner)
    def _():
        pl.semaphore_wait(barrier, 2 + ends)

    @pl.when(jnp.logical_not(inner))
    def _():
        pl.semaphore_wait(barrier, 2 + (depth > 1))

    me = row * 2 + y

    def slot_of(zz, xx, yy):
        return (zz * 2 + xx) * 2 + yy

    sent = []

    def descriptor(number, slot, own, way, target=None):
        start, size, _ = plan[number]
        span = pl.ds(start, size)
        source = own_ref.at[span] if own else out_ref.at[slot, span]
        return pltpu.make_async_remote_copy(
            src_ref=source,
            dst_ref=out_ref.at[slot, span],
            send_sem=send_sem.at[way, slot, number],
            recv_sem=recv_sem.at[slot, number],
            device_id=where[way] if target is None else target,
            device_id_type=MESH,
        )

    def guarded(cond, fn):
        if cond is None:
            fn()
        else:
            pl.when(cond)(fn)

    def both(a, b):
        if a is None:
            return b
        if b is None:
            return a
        return jnp.logical_and(a, b)

    def send(number, slot, own, way, cond):
        cond = both(cond, exists.get(way))
        guarded(cond, lambda: descriptor(number, slot, own, way).start())
        sent.append((number, slot, own, way, cond))

    def arrived(number, slot, cond):
        guarded(cond, lambda: descriptor(number, slot, False, XP).wait_recv())

    local = pltpu.make_async_copy(own_ref, out_ref.at[me], local_sem)
    local.start()

    partner = {"x": XP, "y": YP}

    def coords(flip_x, flip_y):
        return (1 - x if flip_x else x), (1 - y if flip_y else y)

    reach = [0]
    for k in range(1, depth):
        reach += [-k, k]

    def near(dz):
        if dz == 0:
            return None
        return z + dz >= 0 if dz < 0 else z + dz < depth

    def onward_z(number, slot, own, dz, cond):
        if dz <= 0:
            send(number, slot, own, UP, cond)
        if dz >= 0:
            send(number, slot, own, DOWN, cond)

    def z_first(number, order, dz, level):
        first, second = order[1], order[2]
        flips = {0: "", 1: first, 2: second, 3: "xy"}[level]
        xx, yy = coords("x" in flips, "y" in flips)
        slot = slot_of(z + dz, xx, yy)
        own = level == 0 and dz == 0
        cond = near(dz)
        if not own:
            arrived(number, slot, cond)
        if level == 0:
            onward_z(number, slot, own, dz, cond)
            send(number, slot, own, partner[first], cond)
            send(number, slot, own, partner[second], cond)
        elif level == 1:
            send(number, slot, own, partner[second], cond)

    def z_last(number, order, dz, level):
        first, second = order[0], order[1]
        flips = {0: "", 1: first, 2: second, 3: "xy"}[level]
        xx, yy = coords("x" in flips, "y" in flips)
        slot = slot_of(z + dz, xx, yy)
        own = level == 0 and dz == 0
        cond = near(dz)
        if not own:
            arrived(number, slot, cond)
        onward_z(number, slot, own, dz, cond)
        if dz == 0:
            if level == 0:
                send(number, slot, own, partner[first], cond)
            if level in (0, 1):
                send(number, slot, own, partner[second], cond)

    def handle(number, dz, level):
        order = plan[number][2]
        (z_first if order[0] == "z" else z_last)(number, order, dz, level)

    numbers = range(len(plan))
    events = []
    for number in numbers:
        for position, dz in enumerate(reach):
            hop = (position + 1) // 2
            for level in range(4):
                events.append((2 * hop + (0, 2, 2, 4)[level], number, position, level, dz))
    events.sort(key=lambda e: e[:4])
    for _, number, _, level, dz in events:
        handle(number, dz, level)
    for number, slot, own, way, cond in sent:
        guarded(cond, lambda: descriptor(number, slot, own, way).wait_send())
    local.wait()


def gather(own, row_size, col_size):
    depth = row_size // 2
    blocks = own.shape[0]
    plan = gather_plan(blocks)
    devices = row_size * col_size
    return pl.pallas_call(
        functools.partial(gather_kernel, depth, plan),
        out_shape=jax.ShapeDtypeStruct((devices,) + own.shape, own.dtype),
        in_specs=[pl.BlockSpec(memory_space=pl.ANY)],
        out_specs=pl.BlockSpec(memory_space=pl.ANY),
        scratch_shapes=[
            pltpu.SemaphoreType.DMA((4, devices, len(plan))),
            pltpu.SemaphoreType.DMA((devices, len(plan))),
            pltpu.SemaphoreType.DMA,
        ],
        compiler_params=pltpu.CompilerParams(collective_id=0, has_side_effects=True),
        name="gather",
    )(own)


def product_kernel(snodes, width, tile, table_ref, gate_ref, half_ref, a_ref, *rest):
    piece_refs = rest[: snodes * width]
    out_ref, stack_ref, total_ref = rest[snodes * width :]
    step = pl.program_id(0)
    for b in range(width):
        for s in range(snodes):
            stack_ref[b * tile : (b + 1) * tile, s * tile : (s + 1) * tile] = piece_refs[
                b * snodes + s
            ][...]

    @pl.when(step == 0)
    def _():
        total_ref[...] = jnp.zeros_like(total_ref)

    row_tiles = a_ref.shape[0] // tile
    for i in range(row_tiles):
        rows = slice(i * tile, (i + 1) * tile)
        parts = []
        for b in range(width):
            gate = gate_ref[half_ref[0] * row_tiles + i, step * width + b]
            part = a_ref[rows, b * tile : (b + 1) * tile]
            parts.append(part * gate.astype(jnp.float32).astype(part.dtype))
        total_ref[rows, :] += jnp.dot(
            jnp.concatenate(parts, axis=1), stack_ref[...], preferred_element_type=jnp.float32
        )

    @pl.when(step == pl.num_programs(0) - 1)
    def _():
        for i in range(row_tiles):
            rows = slice(i * tile, (i + 1) * tile)
            out_ref[:, rows] = (-total_ref[rows, :]).T.astype(out_ref.dtype)


def product(table, gate, half, ancestor_inverse, pieces, shares, snodes, tile, dtype):
    local_rows, local_cols = ancestor_inverse.shape
    rows = local_rows // shares
    col_blocks = local_cols // tile
    width = max(w for w in range(1, 6) if col_blocks % w == 0)

    def piece_spec(b, s):
        return pl.BlockSpec(
            (pl.Squeezed(), tile, tile),
            lambda k, table_ref, gate_ref, half_ref: (table_ref[s, k * width + b], 0, 0),
        )

    return pl.pallas_call(
        functools.partial(product_kernel, snodes, width, tile),
        out_shape=jax.ShapeDtypeStruct((snodes * tile, rows), dtype),
        grid_spec=pltpu.PrefetchScalarGridSpec(
            num_scalar_prefetch=3,
            grid=(col_blocks // width,),
            in_specs=[
                pl.BlockSpec((rows, width * tile), lambda k, t, g, half_ref: (half_ref[0], k))
            ]
            + [piece_spec(b, s) for b in range(width) for s in range(snodes)],
            out_specs=pl.BlockSpec((snodes * tile, rows), lambda k, t, g, h: (0, 0)),
            scratch_shapes=[
                pltpu.VMEM((width * tile, snodes * tile), jnp.bfloat16),
                pltpu.VMEM((rows, snodes * tile), jnp.float32),
            ],
        ),
        compiler_params=pltpu.CompilerParams(
            dimension_semantics=("arbitrary",), vmem_limit_bytes=56 * 1024 * 1024
        ),
        cost_estimate=pl.CostEstimate(
            flops=2 * rows * local_cols * snodes * tile,
            bytes_accessed=2 * rows * local_cols,
            transcendentals=0,
        ),
        name="product",
    )(table, gate, half, ancestor_inverse, *([pieces] * (snodes * width)))


def fast(ancestor_inverse, fill_mask, block_order, l_rows, diag_inverse):
    row_index = lax.axis_index("row")
    col_index = lax.axis_index("col")
    row_size = lax.axis_size("row")
    col_size = lax.axis_size("col")
    local_rows, local_cols = ancestor_inverse.shape
    snodes, tile = diag_inverse.shape[:2]
    row_blocks = local_rows // tile
    col_blocks = local_cols // tile
    held = l_rows.shape[1] // tile
    normed = jnp.einsum(
        "sxy,syz->sxz", l_rows, diag_inverse, preferred_element_type=jnp.float32
    ).astype(jnp.bfloat16)
    own = normed.reshape(snodes * held, tile, tile)
    pieces = gather(own, row_size, col_size).reshape(-1, tile, tile)

    wanted = col_index * col_blocks + jnp.arange(col_blocks, dtype=jnp.int32)
    packed = jnp.arange(block_order.shape[1], dtype=jnp.int32)
    place = jnp.sum(
        jnp.where(block_order[:, None, :] == wanted[None, :, None], packed[None, None, :], 0), axis=2
    )
    table = (
        (place // held) * (snodes * held)
        + jnp.arange(snodes, dtype=jnp.int32)[:, None] * held
        + place % held
    ).astype(jnp.int32)
    gate = lax.dynamic_slice(
        fill_mask, (row_index * row_blocks, col_index * col_blocks), (row_blocks, col_blocks)
    )

    def share(half, dtype):
        return product(
            table, gate, half.reshape(1).astype(jnp.int32), ancestor_inverse, pieces,
            col_size, snodes, tile, dtype,
        )

    theirs = share(1 - col_index, jnp.bfloat16)
    received = lax.ppermute(theirs, "col", [(0, 1), (1, 0)])
    mine = share(col_index, jnp.float32)
    total = (mine + received.astype(jnp.float32)).astype(jnp.bfloat16)
    return total.reshape(snodes, tile, local_rows // col_size)


def plain(ancestor_inverse, fill_mask, block_order, l_rows, diag_inverse):
    row_index = lax.axis_index("row")
    col_index = lax.axis_index("col")
    local_rows, local_cols = ancestor_inverse.shape
    snode_count, tile_size = diag_inverse.shape[:2]
    block_count = fill_mask.shape[0]
    row_blocks = local_rows // tile_size
    col_blocks = local_cols // tile_size
    normed = jnp.einsum(
        "sxy,syz->sxz", l_rows, diag_inverse, preferred_element_type=jnp.float32
    ).astype(jnp.bfloat16)
    wanted = col_index * col_blocks + jnp.arange(col_blocks, dtype=jnp.int32)
    everything = lax.all_gather(normed, ("row", "col"), axis=1, tiled=True)
    pieces = everything.reshape(snode_count, block_count, tile_size, tile_size)
    selector = (block_order[:, None, :] == wanted[None, :, None]).astype(jnp.bfloat16)
    columns = jnp.einsum(
        "saq,sqxy->saxy", selector, pieces, preferred_element_type=jnp.float32
    ).astype(jnp.bfloat16)
    stacked = columns.transpose(1, 2, 0, 3).reshape(local_cols, snode_count * tile_size)
    tile_gate = lax.dynamic_slice(
        fill_mask, (row_index * row_blocks, col_index * col_blocks), (row_blocks, col_blocks)
    ).astype(jnp.bfloat16)
    masked = (
        ancestor_inverse.reshape(row_blocks, tile_size, col_blocks, tile_size)
        * tile_gate[:, None, :, None]
    ).reshape(local_rows, local_cols)
    share_rows = local_rows // lax.axis_size("col")
    own_rows = lax.psum_scatter(
        (-jnp.dot(masked, stacked, preferred_element_type=jnp.float32)).astype(jnp.bfloat16),
        "col",
        scatter_dimension=0,
        tiled=True,
    ).astype(jnp.float32)
    return (
        own_rows.reshape(share_rows, snode_count, tile_size).transpose(1, 2, 0).astype(jnp.bfloat16)
    )


def per_device(ancestor_inverse, fill_mask, block_order, l_rows, diag_inverse):
    tile = diag_inverse.shape[1]
    col_size = lax.axis_size("col")
    if (
        col_size == 2
        and lax.axis_size("row") % 2 == 0
        and l_rows.shape[1] % tile == 0
        and ancestor_inverse.shape[0] % (col_size * tile) == 0
    ):
        return fast(ancestor_inverse, fill_mask, block_order, l_rows, diag_inverse)
    return plain(ancestor_inverse, fill_mask, block_order, l_rows, diag_inverse)


def solution(mesh):
    return jax.shard_map(
        per_device,
        mesh=mesh,
        in_specs=(
            P(("snode", "row"), "col"),
            P("snode", None),
            P("snode", None),
            P("snode", ("row", "col"), None),
            P("snode", None, None),
        ),
        out_specs=P("snode", None, ("row", "col")),
        check_vma=False,
    )
```
